128 devices in a mesh: freq: 32 (over y_lo, x, z), blk: 4 (over y_hi, core).
Axes of the slice: x: 4, y: 4 (y_hi: 2, y_lo: 2; y = y_hi * 2 + y_lo), z: 4, core: 2. Of those that a mesh axis runs over, the one named last changes fastest.
Arguments:
- voltages: int32 [2, 512, 262144], P(None, 'blk', 'freq'), may hold values from -8 to 7
- taps: int32 [4, 1024], replicated, may hold values from -32 to 127
Outputs:
- visibilities: float32 [2, 1024, 512, 512], P(None, 'freq', 'blk')
The draws below stay inside these ranges and needn't reach their ends.
All inputs are finite; a program needn't handle non-finite values.
Results may differ from the reference program's by a relative error of at most 0.00065.
Values may be sent and summed in bfloat16 or wider, within the bound.
A program may use at most 128 MiB of HBM per device.

```python
import math
import jax
import jax.numpy as jnp
from jax import lax

C = 1024
TAPS = 4
INPUTS = 512
SPECTRA = 256
SAMPLES = 262144
N_FREQ = 32


def plant(entries, key, smallest, largest):
    index_at = [jax.random.randint(jax.random.fold_in(key, axis), (), 0, length) for axis, length in enumerate(entries.shape)]
    longest = entries.shape.index(max(entries.shape))
    next_to = index_at[:longest] + [(index_at[longest] + 1) % entries.shape[longest]] + index_at[longest + 1:]
    return entries.at[tuple(index_at)].set(smallest).at[tuple(next_to)].set(largest)


def setup_inputs(seed: int = 0) -> dict:
    seeds = jax.random.split(jax.random.key(seed), 3)
    voltages = plant(jax.random.randint(seeds[0], (2, INPUTS, SAMPLES), -8, 8), jax.random.fold_in(seeds[0], 1), -8, 7).astype(jnp.int32)
    taps = plant(jax.random.randint(seeds[1], (TAPS, C), -32, 128), jax.random.fold_in(seeds[1], 1), -32, 127).astype(jnp.int32)
    return {"voltages": voltages, "taps": taps}


def dft_table(channels):
    row_index = lax.broadcasted_iota(jnp.int32, (channels, channels), 0)
    col_index = lax.broadcasted_iota(jnp.int32, (channels, channels), 1)
    phase = (row_index * col_index % channels).astype(jnp.float32) * (2.0 * math.pi / channels)
    factor = 1.0 / math.sqrt(channels)
    cosine = (jnp.cos(phase) * factor).astype(jnp.bfloat16)
    sine = (jnp.sin(phase) * factor).astype(jnp.bfloat16)
    upper = jnp.concatenate([cosine, -sine], axis=1)
    lower = jnp.concatenate([sine, cosine], axis=1)
    return jnp.concatenate([upper, lower], axis=0)

def reference(voltages, taps):
    volts = voltages.astype(jnp.float32).reshape(2, INPUTS, SPECTRA, C).transpose(2, 1, 0, 3)
    coeffs = taps.astype(jnp.float32) / 1024.0
    padded = jnp.pad(volts, ((TAPS - 1, 0), (0, 0), (0, 0), (0, 0)))
    filtered = jnp.zeros((SPECTRA, INPUTS, 2, C), jnp.float32)
    for tap in range(TAPS):
        filtered = filtered + coeffs[tap][None, None, None, :] * padded[tap:tap + SPECTRA]
    weighted = lax.optimization_barrier(filtered.astype(jnp.bfloat16)).astype(jnp.float32)
    table = dft_table(C).astype(jnp.float32)
    spectra = jnp.dot(weighted.reshape(SPECTRA * INPUTS, 2 * C), table, precision=lax.Precision.HIGHEST, preferred_element_type=jnp.float32)
    spectra = lax.optimization_barrier(spectra.astype(jnp.bfloat16)).astype(jnp.float32)
    group = C // N_FREQ
    blocks = spectra.reshape(SPECTRA, INPUTS, 2, N_FREQ, group).transpose(3, 0, 1, 2, 4)
    factor = 1.0 / math.sqrt(SPECTRA)

    def correlate(tile):
        rotated = jnp.stack([-tile[:, :, 1], tile[:, :, 0]], axis=2)
        partner = jnp.stack([tile, rotated], axis=2)
        return jnp.einsum('sirc,sjorc->ocij', tile, partner, precision=lax.Precision.HIGHEST) * factor
    result = lax.map(correlate, blocks)
    return result.transpose(1, 0, 2, 3, 4).reshape(2, C, INPUTS, INPUTS)
```

```python
import functools
import math

import jax
import jax.numpy as jnp
import ml_dtypes
import numpy as np
from jax import lax
from jax.experimental import pallas as pl
from jax.experimental.pallas import tpu as pltpu
from jax.sharding import PartitionSpec as P

MESH = pl.DeviceIdType.MESH
CHANNELS = 1024
HALF = CHANNELS // 2
INPUTS = 128
FRAMES = 8
GROUP = 32
PITCH = CHANNELS + 8
CHUNK = 256
LAG = 8


def fourier_rows():
    n = np.arange(CHANNELS)
    k = np.arange(HALF)
    step = np.float32(2.0 * math.pi / CHANNELS)
    scale = np.float32(1.0 / math.sqrt(CHANNELS))
    phase = (np.outer(k, n) % CHANNELS).astype(np.float32) * step
    cosine = np.cos(phase) * scale
    sine = np.sin(phase) * scale
    sine[0] = np.cos((HALF * n % CHANNELS).astype(np.float32) * step) * scale
    both = np.stack([cosine.reshape(-1, CHUNK, CHANNELS), sine.reshape(-1, CHUNK, CHANNELS)], axis=1)
    return both.reshape(CHANNELS, CHANNELS).astype(ml_dtypes.bfloat16)


def position():
    f = lax.axis_index("freq")
    b = lax.axis_index("blk")
    return (f // 4) % 4, (b // 2) * 2 + f // 16, f % 4, b % 2


def device(x, y, z, c):
    return ((y % 2) * 16 + x * 4 + z, (y // 2) * 2 + c)


def offset(i):
    return i % 4, (i // 4 + i) % 4


def turn_kernel(
    volts, taps, table_hbm, out,
    frames, halo_out, halo_in, coeffs, weighted, table, spectra, outbox, inbox,
    load_sem, table_sem, halo_send, halo_recv, plane_send, plane_recv,
    y_send, y_recv, core_send, core_recv, dup_send, dup_recv, keep_sem,
):
    f = lax.axis_index("freq")
    block = lax.axis_index("blk")
    x, y, z, c = position()
    y_lo = y % 2
    here = x * 4 + z
    up = device(x, (y + 1) % 4, z, c)
    down = device(x, (y + 3) % 4, z, c)
    across = device(x, (y + 2) % 4, z, c)
    twin = device(x, y, z, 1 - c)
    after = ((f + 1) % 32, block)
    before = ((f + 31) % 32, block)

    def plane(i, sign):
        dx, dz = offset(i)
        px = (x + 4 + sign * dx) % 4
        pz = (z + 4 + sign * dz) % 4
        return px * 4 + pz, device(px, y, pz, c)

    barrier = pltpu.get_barrier_semaphore()
    for partner in (up, down, across, twin, after, before):
        pl.semaphore_signal(barrier, inc=1, device_id=partner, device_id_type=MESH)

    def greet(i, carry):
        pl.semaphore_signal(barrier, inc=1, device_id=plane(i, 1)[1], device_id_type=MESH)
        return carry

    lax.fori_loop(1, 16, greet, 0)

    def load(s):
        return pltpu.make_async_copy(
            volts.at[:, :, pl.ds(s * CHANNELS, CHANNELS)], frames.at[s], load_sem.at[s]
        )

    table_copy = pltpu.make_async_copy(table_hbm, table, table_sem)
    for s in (5, 6, 7, 4, 3, 2, 1):
        load(s).start()
    table_copy.start()
    load(0).start()

    coeffs[...] = taps[...].astype(jnp.float32) * (1.0 / 1024.0)

    for j in range(3):
        load(5 + j).wait()

        def narrow(t, carry):
            rows = pl.ds(pl.multiple_of(t * 16, 16), 16)
            for r in range(2):
                halo_out[j, r, rows, :] = frames[5 + j, r, rows, :].astype(jnp.bfloat16)
            return carry

        lax.fori_loop(0, INPUTS // 16, narrow, 0)

    pl.semaphore_wait(barrier, 21)
    halo = pltpu.make_async_remote_copy(
        src_ref=halo_out, dst_ref=halo_in, send_sem=halo_send, recv_sem=halo_recv,
        device_id=after, device_id_type=MESH,
    )
    halo.start()

    def filter_half(earlier, first):
        def body(t, carry):
            rows = pl.ds(pl.multiple_of(t * 16, 16), 16)
            for r in range(2):
                for n in range(0, CHANNELS, 256):
                    cols = slice(n, n + 256)
                    seen = [earlier(j, r, rows, cols) for j in range(3)]
                    seen += [frames[first + j, r, rows, cols].astype(jnp.float32) for j in range(4)]
                    scale = [jnp.broadcast_to(coeffs[k : k + 1, cols], (16, 256)) for k in range(4)]
                    for s in range(4):
                        total = scale[0] * seen[s]
                        for k in range(1, 4):
                            total = total + scale[k] * seen[s + k]
                        into = pl.ds(pl.multiple_of(r * INPUTS + t * 16, 16), 16)
                        weighted[s, into, cols] = total.astype(jnp.bfloat16)
            return carry

        lax.fori_loop(0, INPUTS // 16, body, 0)

    def transform_half():
        def body(s, carry):
            rhs = weighted[s]
            re = pl.multiple_of(s * PITCH, 8)
            im = pl.multiple_of((4 + s) * PITCH, 8)
            for q in range(HALF // CHUNK):
                got = lax.dot_general(
                    table[q * 2 * CHUNK : (q + 1) * 2 * CHUNK, :], rhs, (((1,), (1,)), ((), ())),
                    preferred_element_type=jnp.float32,
                )
                a, b = got[:CHUNK, :INPUTS], got[CHUNK:, :INPUTS]
                cc, d = got[:CHUNK, INPUTS:], got[CHUNK:, INPUTS:]
                k = q * CHUNK
                spectra[pl.ds(re + k, CHUNK), :] = a + d
                spectra[pl.ds(im + k, CHUNK), :] = cc - b
                spectra[pl.ds(re + HALF + k, CHUNK), :] = a - d
                spectra[pl.ds(im + HALF + k, CHUNK), :] = cc + b
                if q == 0:
                    spectra[pl.ds(re, 1), :] = a[:1]
                    spectra[pl.ds(im, 1), :] = cc[:1]
                    spectra[pl.ds(re + CHANNELS, 1), :] = b[:1]
                    spectra[pl.ds(im + CHANNELS, 1), :] = d[:1]
            return carry

        lax.fori_loop(0, 4, body, 0)

    def gather(g, into):
        for k in range(GROUP):
            low = spectra[pl.ds(g * GROUP + k, 8, stride=PITCH), :]
            into[0, k] = low.astype(jnp.bfloat16)
            high = spectra[pl.ds(CHANNELS - g * GROUP - k, 8, stride=PITCH), :]
            into[1, k] = high.astype(jnp.bfloat16)

    def plane_copy(h, i):
        g, to = plane(i, 1)
        return pltpu.make_async_remote_copy(
            src_ref=outbox.at[h, g], dst_ref=inbox.at[h, here], send_sem=plane_send.at[h],
            recv_sem=plane_recv.at[h, here], device_id=to, device_id_type=MESH,
        )

    def send_half(h):
        def body(i, carry):
            gather(plane(i, 1)[0], outbox.at[h, plane(i, 1)[0]])
            plane_copy(h, i).start()
            return carry

        lax.fori_loop(1, 16, body, 0)
        gather(here, inbox.at[h, here])

    def forward(h, i):
        j = plane(i, -1)[0]

        @pl.when(i > 0)
        def _():
            pltpu.make_async_remote_copy(
                src_ref=inbox.at[h, j], dst_ref=inbox.at[h, j], send_sem=plane_send.at[h],
                recv_sem=plane_recv.at[h, j], device_id=twin, device_id_type=MESH,
            ).wait_recv()

        theirs = inbox.at[h, j, 1 - y_lo]
        ours = inbox.at[h, j, y_lo]
        slot = out.at[block, h, y_lo * 16 + j]
        for way, (to, chunk) in enumerate(((up, theirs), (down, theirs), (across, ours))):
            pltpu.make_async_remote_copy(
                src_ref=chunk, dst_ref=slot, send_sem=y_send.at[way], recv_sem=y_recv.at[way, h, j],
                device_id=to, device_id_type=MESH,
            ).start()
        pltpu.make_async_remote_copy(
            src_ref=ours, dst_ref=slot, send_sem=core_send, recv_sem=core_recv,
            device_id=twin, device_id_type=MESH,
        ).start()
        pltpu.make_async_copy(ours, slot, keep_sem).start()

    def arrival(way, h, j):
        sender = (y + 3 - 2 * way) % 4 if way < 2 else (y + 2) % 4
        return out.at[(sender // 2) * 2 + c, h, (sender % 2) * 16 + j]

    def duplicate(h, i):
        j = plane(i, -1)[0]
        for way in range(3):
            slot = arrival(way, h, j)
            pltpu.make_async_remote_copy(
                src_ref=slot, dst_ref=slot, send_sem=y_send.at[way], recv_sem=y_recv.at[way, h, j],
                device_id=twin, device_id_type=MESH,
            ).wait_recv()
            pltpu.make_async_remote_copy(
                src_ref=slot, dst_ref=slot, send_sem=dup_send.at[way], recv_sem=dup_recv.at[way],
                device_id=twin, device_id_type=MESH,
            ).start()

    for s in (4, 3, 2, 1):
        load(s).wait()
    filter_half(lambda j, r, rows, cols: frames[1 + j, r, rows, cols].astype(jnp.float32), 4)
    table_copy.wait()
    transform_half()
    send_half(0)

    def first(i, carry):
        forward(0, i)

        @pl.when(i >= LAG)
        def _():
            duplicate(0, i - LAG)

        return carry

    lax.fori_loop(0, 16, first, 0)

    load(0).wait()
    halo.wait()
    live = jnp.where(f > 0, 1.0, 0.0).astype(jnp.float32)
    filter_half(lambda j, r, rows, cols: halo_in[j, r, rows, cols].astype(jnp.float32) * live, 0)
    transform_half()
    send_half(1)

    def second(i, carry):
        forward(1, i)

        @pl.when(i < LAG)
        def _():
            duplicate(0, i + 16 - LAG)

        @pl.when(i >= LAG)
        def _():
            duplicate(1, i - LAG)

        return carry

    lax.fori_loop(0, 16, second, 0)

    def last(i, carry):
        duplicate(1, i)
        return carry

    lax.fori_loop(16 - LAG, 16, last, 0)

    def whole(ref, send_sem, recv_sem):
        return pltpu.make_async_remote_copy(
            src_ref=ref, dst_ref=ref, send_sem=send_sem, recv_sem=recv_sem,
            device_id=twin, device_id_type=MESH,
        )

    for h in range(2):
        whole(outbox.at[h, pl.ds(0, 15)], plane_send.at[h], plane_recv.at[0, 0]).wait_send()
    part = out.at[0, 0]
    for way in range(3):
        whole(part, y_send.at[way], core_recv).wait_send()
        whole(part, dup_send.at[way], core_recv).wait_send()
        whole(part, dup_send.at[way], dup_recv.at[way]).wait_recv()
    whole(part, core_send, core_recv).wait_send()
    whole(part, core_send, core_recv).wait_recv()
    pltpu.make_async_copy(part, part, keep_sem).wait()


def corner_turn(voltages, taps, table):
    bf16 = jnp.bfloat16
    dma = pltpu.SemaphoreType.DMA
    return pl.pallas_call(
        turn_kernel,
        out_shape=jax.ShapeDtypeStruct((4, 2, 32, GROUP, 8, INPUTS), bf16),
        in_specs=[
            pl.BlockSpec(memory_space=pl.ANY),
            pl.BlockSpec(memory_space=pltpu.VMEM),
            pl.BlockSpec(memory_space=pl.ANY),
        ],
        out_specs=pl.BlockSpec(memory_space=pl.ANY),
        scratch_shapes=[
            pltpu.VMEM((FRAMES, 2, INPUTS, CHANNELS), jnp.int32),
            pltpu.VMEM((3, 2, INPUTS, CHANNELS), bf16),
            pltpu.VMEM((3, 2, INPUTS, CHANNELS), bf16),
            pltpu.VMEM((4, CHANNELS), jnp.float32),
            pltpu.VMEM((4, 2 * INPUTS, CHANNELS), bf16),
            pltpu.VMEM((CHANNELS, CHANNELS), bf16),
            pltpu.VMEM((8 * PITCH, INPUTS), jnp.float32),
            pltpu.VMEM((2, 16, 2, GROUP, 8, INPUTS), bf16),
            pltpu.VMEM((2, 16, 2, GROUP, 8, INPUTS), bf16),
            dma((FRAMES,)), dma, dma, dma, dma((2,)), dma((2, 16)),
            dma((3,)), dma((3, 2, 16)), dma, dma, dma((3,)), dma((3,)), dma,
        ],
        compiler_params=pltpu.CompilerParams(
            collective_id=0, has_side_effects=True, vmem_limit_bytes=56 << 20
        ),
        name="corner_turn",
    )(voltages, taps, table)


def correlate_kernel(count, tiles, visible):
    me = lax.axis_index("blk")
    part = lax.broadcasted_iota(jnp.int32, (1, 8, INPUTS), 1)
    sign = jnp.where(part < 4, 0.0625, -0.0625).astype(jnp.float32)
    rows = 64 * 8
    for k in range(count):
        mine = tiles[me, :, k].astype(jnp.float32)
        rotated = pltpu.roll(mine, 4, axis=1) * sign
        left = jnp.concatenate(
            [(mine * 0.0625).reshape(rows, INPUTS), rotated.reshape(rows, INPUTS)], axis=1
        ).astype(jnp.bfloat16)
        for b in range(0, 4, 2):
            right = jnp.concatenate(
                [tiles[b, :, k].reshape(rows, INPUTS), tiles[b + 1, :, k].reshape(rows, INPUTS)], axis=1
            )
            both = lax.dot_general(
                left, right, (((0,), (0,)), ((), ())), preferred_element_type=jnp.float32
            )
            visible[0, k, :, b * INPUTS : (b + 2) * INPUTS] = both[:INPUTS]
            visible[1, k, :, b * INPUTS : (b + 2) * INPUTS] = both[INPUTS:]


def correlate(tiles, count=8):
    return pl.pallas_call(
        functools.partial(correlate_kernel, count),
        grid=(GROUP // count,),
        in_specs=[pl.BlockSpec((4, 64, count, 8, INPUTS), lambda k: (0, 0, k, 0, 0))],
        out_specs=pl.BlockSpec((2, count, INPUTS, 4 * INPUTS), lambda k: (0, k, 0, 0)),
        out_shape=jax.ShapeDtypeStruct((2, GROUP, INPUTS, 4 * INPUTS), jnp.float32),
        compiler_params=pltpu.CompilerParams(vmem_limit_bytes=40 << 20),
        name="correlate",
    )(tiles)


def local(voltages, taps):
    table = jnp.asarray(fourier_rows())
    tiles = corner_turn(voltages, taps, table)
    return correlate(tiles.reshape(4, 64, GROUP, 8, INPUTS))


def solution(mesh):
    in_specs = (P(None, "blk", "freq"), P())
    out_specs = P(None, "freq", "blk", None)
    return jax.shard_map(local, mesh=mesh, in_specs=in_specs, out_specs=out_specs, check_vma=False)
```

```python
import functools
import math

import jax
import jax.numpy as jnp
import ml_dtypes
import numpy as np
from jax import lax
from jax.experimental import pallas as pl
from jax.experimental.pallas import tpu as pltpu
from jax.sharding import PartitionSpec as P

MESH = pl.DeviceIdType.MESH
CHANNELS = 1024
HALF = CHANNELS // 2
INPUTS = 128
FRAMES = 8
GROUP = 32
PITCH = CHANNELS + 8
CHUNK = 256
FIRST = 7
AHEAD = 4
LAG = 8


def fourier_rows():
    n = np.arange(CHANNELS)
    k = np.arange(HALF)
    step = np.float32(2.0 * math.pi / CHANNELS)
    scale = np.float32(1.0 / math.sqrt(CHANNELS))
    phase = (np.outer(k, n) % CHANNELS).astype(np.float32) * step
    cosine = np.cos(phase) * scale
    sine = np.sin(phase) * scale
    sine[0] = np.cos((HALF * n % CHANNELS).astype(np.float32) * step) * scale
    both = np.stack([cosine.reshape(-1, CHUNK, CHANNELS), sine.reshape(-1, CHUNK, CHANNELS)], axis=1)
    return both.reshape(CHANNELS, CHANNELS).astype(ml_dtypes.bfloat16)


def position():
    f = lax.axis_index("freq")
    b = lax.axis_index("blk")
    return (f // 4) % 4, (b // 2) * 2 + f // 16, f % 4, b % 2


def device(x, y, z, c):
    return ((y % 2) * 16 + x * 4 + z, (y // 2) * 2 + c)


def offset(i):
    far = (i + 12) // 16
    r = far * (i - 4)
    return (1 - far) * i + far * (r // 3), far * (1 + r % 3)


def turn_kernel(
    volts, taps, table_hbm, out,
    frames, lines, coeffs, weighted, table, spectra, outbox, inbox,
    load_sem, table_sem, halo_send, halo_recv, plane_send, plane_recv,
    y_send, y_recv, core_send, core_recv, dup_send, dup_recv, keep_sem,
):
    f = lax.axis_index("freq")
    block = lax.axis_index("blk")
    x, y, z, c = position()
    y_lo = y % 2
    here = x * 4 + z
    up = device(x, (y + 1) % 4, z, c)
    down = device(x, (y + 3) % 4, z, c)
    across = device(x, (y + 2) % 4, z, c)
    twin = device(x, y, z, 1 - c)
    after = ((f + 1) % 32, block)
    before = ((f + 31) % 32, block)
    needs_us = ((f + 33 - 2 * c) % 32, block)

    def plane(i, sign):
        dx, dz = offset(i)
        px = (x + 4 + sign * dx) % 4
        pz = (z + 4 + sign * dz) % 4
        return px * 4 + pz, device(px, y, pz, c)

    barrier = pltpu.get_barrier_semaphore()
    for partner in (up, down, across, twin, after, before):
        pl.semaphore_signal(barrier, inc=1, device_id=partner, device_id_type=MESH)

    def greet(i, carry):
        pl.semaphore_signal(barrier, inc=1, device_id=plane(i, 1)[1], device_id_type=MESH)
        return carry

    lax.fori_loop(1, 16, greet, 0)

    def load(p):
        first = pl.multiple_of(((p + 5) % 8) * CHANNELS, CHANNELS)
        return pltpu.make_async_copy(
            volts.at[:, :, pl.ds(first, CHANNELS)], frames.at[p], load_sem.at[p]
        )

    def fetch(t, carry):
        load((3 * c + t) % 8).start()
        return carry

    table_copy = pltpu.make_async_copy(table_hbm, table, table_sem)
    lax.fori_loop(0, 8, fetch, 0)
    table_copy.start()

    coeffs[...] = taps[...].astype(jnp.float32) * (1.0 / 1024.0)

    def narrow(t, carry):
        p = (3 * c + t) % 8
        load(p).wait()

        def body(i, carry):
            rows = pl.ds(pl.multiple_of(i * 16, 16), 16)
            for r in range(2):
                lines[0, p, r, rows, :] = frames[p, r, rows, :].astype(jnp.bfloat16)
            return carry

        return lax.fori_loop(0, INPUTS // 16, body, carry)

    lax.fori_loop(0, 4, narrow, 0)
    pl.semaphore_wait(barrier, 21)
    theirs_first = pl.ds(3 * c, 4)
    halo = pltpu.make_async_remote_copy(
        src_ref=lines.at[0, theirs_first], dst_ref=lines.at[1, theirs_first], send_sem=halo_send,
        recv_sem=halo_recv, device_id=needs_us, device_id_type=MESH,
    )
    halo.start()
    lax.fori_loop(4, 8, narrow, 0)

    def filter_half(frame):
        def body(t, carry):
            rows = pl.ds(pl.multiple_of(t * 16, 16), 16)
            for r in range(2):
                for n in range(0, CHANNELS, 256):
                    cols = slice(n, n + 256)
                    seen = [frame(j, r, rows, cols) for j in range(7)]
                    scale = [jnp.broadcast_to(coeffs[k : k + 1, cols], (16, 256)) for k in range(4)]
                    for s in range(4):
                        total = scale[0] * seen[s]
                        for k in range(1, 4):
                            total = total + scale[k] * seen[s + k]
                        into = pl.ds(pl.multiple_of(r * INPUTS + t * 16, 16), 16)
                        weighted[s, into, cols] = total.astype(jnp.bfloat16)
            return carry

        lax.fori_loop(0, INPUTS // 16, body, 0)

    def late_frame(j, r, rows, cols):
        return frames[(4 + j) % 8, r, rows, cols].astype(jnp.float32)

    live = jnp.where((f + 31 * c) % 62 > 0, 1.0, 0.0).astype(jnp.float32)

    def early_frame(j, r, rows, cols):
        if j < 3:
            return lines[1 - c, j, r, rows, cols].astype(jnp.float32) * live
        return lines[c, j, r, rows, cols].astype(jnp.float32)

    def transform(s):
        rhs = weighted[s]
        re = pl.multiple_of(s * PITCH, 8)
        im = pl.multiple_of((4 + s) * PITCH, 8)
        for q in range(HALF // CHUNK):
            got = lax.dot_general(
                table[q * 2 * CHUNK : (q + 1) * 2 * CHUNK, :], rhs, (((1,), (1,)), ((), ())),
                preferred_element_type=jnp.float32,
            )
            a, b = got[:CHUNK, :INPUTS], got[CHUNK:, :INPUTS]
            cc, d = got[:CHUNK, INPUTS:], got[CHUNK:, INPUTS:]
            k = q * CHUNK
            spectra[pl.ds(re + k, CHUNK), :] = a + d
            spectra[pl.ds(im + k, CHUNK), :] = cc - b
            spectra[pl.ds(re + HALF + k, CHUNK), :] = a - d
            spectra[pl.ds(im + HALF + k, CHUNK), :] = cc + b
            if q == 0:
                spectra[pl.ds(re, 1), :] = a[:1]
                spectra[pl.ds(im, 1), :] = cc[:1]
                spectra[pl.ds(re + CHANNELS, 1), :] = b[:1]
                spectra[pl.ds(im + CHANNELS, 1), :] = d[:1]

    def gather(g, into):
        for k in range(GROUP):
            low = spectra[pl.ds(g * GROUP + k, 8, stride=PITCH), :]
            into[0, k] = low.astype(jnp.bfloat16)
            high = spectra[pl.ds(CHANNELS - g * GROUP - k, 8, stride=PITCH), :]
            into[1, k] = high.astype(jnp.bfloat16)

    def plane_copy(h, i):
        g, to = plane(i, 1)
        return pltpu.make_async_remote_copy(
            src_ref=outbox.at[h, g], dst_ref=inbox.at[h, here], send_sem=plane_send.at[h],
            recv_sem=plane_recv.at[h, here], device_id=to, device_id_type=MESH,
        )

    def collect(h, i):
        g = plane(i, 1)[0]
        gather(g, outbox.at[h, g])

    def forward(h, i):
        j = plane(i, -1)[0]

        def arrive():
            pltpu.make_async_remote_copy(
                src_ref=inbox.at[h, j], dst_ref=inbox.at[h, j], send_sem=plane_send.at[h],
                recv_sem=plane_recv.at[h, j], device_id=twin, device_id_type=MESH,
            ).wait_recv()

        pl.when(i > 0)(arrive)

        theirs = inbox.at[h, j, 1 - y_lo]
        ours = inbox.at[h, j, y_lo]
        slot = out.at[block, h, (y_lo * 16 + j + h * c) % 32]
        for way, (to, chunk) in enumerate(((up, theirs), (down, theirs), (across, ours))):
            pltpu.make_async_remote_copy(
                src_ref=chunk, dst_ref=slot, send_sem=y_send.at[way], recv_sem=y_recv.at[way, h, j],
                device_id=to, device_id_type=MESH,
            ).start()
        pltpu.make_async_remote_copy(
            src_ref=ours, dst_ref=slot, send_sem=core_send, recv_sem=core_recv,
            device_id=twin, device_id_type=MESH,
        ).start()
        pltpu.make_async_copy(ours, slot, keep_sem).start()

    def arrival(way, h, j):
        sender = (y + 3 - 2 * way) % 4 if way < 2 else (y + 2) % 4
        return out.at[(sender // 2) * 2 + c, h, ((sender % 2) * 16 + j + h * c) % 32]

    def duplicate(h, i):
        j = plane(i, -1)[0]
        for way in range(3):
            slot = arrival(way, h, j)
            pltpu.make_async_remote_copy(
                src_ref=slot, dst_ref=slot, send_sem=y_send.at[way], recv_sem=y_recv.at[way, h, j],
                device_id=twin, device_id_type=MESH,
            ).wait_recv()
            pltpu.make_async_remote_copy(
                src_ref=slot, dst_ref=slot, send_sem=dup_send.at[way], recv_sem=dup_recv.at[way],
                device_id=twin, device_id_type=MESH,
            ).start()

    def steps(first, stop, *bodies):
        def run(i, carry):
            for body in bodies:
                body(i)
            return carry

        lax.fori_loop(first, stop, run, 0)

    def step(k):
        forward(k // 16, k % 16)

        @pl.when(k >= LAG)
        def _():
            duplicate((k - LAG) // 16, (k - LAG) % 16)

    def send(m):
        plane_copy(m // 16, m % 16).start()

    filter_half(late_frame)
    table_copy.wait()
    steps(0, 4, transform)
    gather(here, inbox.at[0, here])
    step(0)
    steps(1, FIRST, lambda i: collect(0, i), send)
    steps(FIRST, 16, lambda i: collect(0, i))
    steps(1, FIRST, step)
    halo.wait_send()
    steps(FIRST, FIRST + AHEAD, send)

    halo.wait_recv()
    filter_half(early_frame)
    steps(0, 4, transform, lambda i: step(FIRST + i))
    steps(FIRST + AHEAD, 16, send)
    gather(here, inbox.at[1, here])
    steps(1, 4, lambda i: collect(1, i), lambda i: send(16 + i))
    steps(4, 16, lambda i: collect(1, i))
    steps(FIRST + 4, FIRST + 16, step, lambda k: send(k + 16 - FIRST))
    steps(FIRST + 16, 32, step)
    steps(32 - LAG, 32, lambda k: duplicate(k // 16, k % 16))

    def whole(ref, send_sem, recv_sem):
        return pltpu.make_async_remote_copy(
            src_ref=ref, dst_ref=ref, send_sem=send_sem, recv_sem=recv_sem,
            device_id=twin, device_id_type=MESH,
        )

    for h in range(2):
        whole(outbox.at[h, pl.ds(0, 15)], plane_send.at[h], plane_recv.at[0, 0]).wait_send()
    part = out.at[0, 0]
    for way in range(3):
        whole(part, y_send.at[way], core_recv).wait_send()
        whole(part, dup_send.at[way], core_recv).wait_send()
        whole(part, dup_send.at[way], dup_recv.at[way]).wait_recv()
    whole(part, core_send, core_recv).wait_send()
    whole(part, core_send, core_recv).wait_recv()
    pltpu.make_async_copy(part, part, keep_sem).wait()


def corner_turn(voltages, taps, table):
    bf16 = jnp.bfloat16
    dma = pltpu.SemaphoreType.DMA
    return pl.pallas_call(
        turn_kernel,
        out_shape=jax.ShapeDtypeStruct((4, 2, 32, GROUP, 8, INPUTS), bf16),
        in_specs=[
            pl.BlockSpec(memory_space=pl.ANY),
            pl.BlockSpec(memory_space=pltpu.VMEM),
            pl.BlockSpec(memory_space=pl.ANY),
        ],
        out_specs=pl.BlockSpec(memory_space=pl.ANY),
        scratch_shapes=[
            pltpu.VMEM((FRAMES, 2, INPUTS, CHANNELS), jnp.int32),
            pltpu.VMEM((2, 8, 2, INPUTS, CHANNELS), bf16),
            pltpu.VMEM((4, CHANNELS), jnp.float32),
            pltpu.VMEM((4, 2 * INPUTS, CHANNELS), bf16),
            pltpu.VMEM((CHANNELS, CHANNELS), bf16),
            pltpu.VMEM((8 * PITCH, INPUTS), jnp.float32),
            pltpu.VMEM((2, 16, 2, GROUP, 8, INPUTS), bf16),
            pltpu.VMEM((2, 16, 2, GROUP, 8, INPUTS), bf16),
            dma((FRAMES,)), dma, dma, dma, dma((2,)), dma((2, 16)),
            dma((3,)), dma((3, 2, 16)), dma, dma, dma((3,)), dma((3,)), dma,
        ],
        compiler_params=pltpu.CompilerParams(
            collective_id=0, has_side_effects=True, vmem_limit_bytes=56 << 20
        ),
        name="corner_turn",
    )(voltages, taps, table)


def correlate_kernel(count, tiles, visible):
    me = lax.axis_index("blk")
    part = lax.broadcasted_iota(jnp.int32, (1, 8, INPUTS), 1)
    sign = jnp.where(part < 4, 0.0625, -0.0625).astype(jnp.float32)
    rows = 64 * 8
    for k in range(count):
        mine = tiles[me, :, k].astype(jnp.float32)
        rotated = pltpu.roll(mine, 4, axis=1) * sign
        left = jnp.concatenate(
            [(mine * 0.0625).reshape(rows, INPUTS), rotated.reshape(rows, INPUTS)], axis=1
        ).astype(jnp.bfloat16)
        for b in range(0, 4, 2):
            right = jnp.concatenate(
                [tiles[b, :, k].reshape(rows, INPUTS), tiles[b + 1, :, k].reshape(rows, INPUTS)], axis=1
            )
            both = lax.dot_general(
                left, right, (((0,), (0,)), ((), ())), preferred_element_type=jnp.float32
            )
            visible[0, k, :, b * INPUTS : (b + 2) * INPUTS] = both[:INPUTS]
            visible[1, k, :, b * INPUTS : (b + 2) * INPUTS] = both[INPUTS:]


def correlate(tiles, count=8):
    return pl.pallas_call(
        functools.partial(correlate_kernel, count),
        grid=(GROUP // count,),
        in_specs=[pl.BlockSpec((4, 64, count, 8, INPUTS), lambda k: (0, 0, k, 0, 0))],
        out_specs=pl.BlockSpec((2, count, INPUTS, 4 * INPUTS), lambda k: (0, k, 0, 0)),
        out_shape=jax.ShapeDtypeStruct((2, GROUP, INPUTS, 4 * INPUTS), jnp.float32),
        compiler_params=pltpu.CompilerParams(vmem_limit_bytes=40 << 20),
        name="correlate",
    )(tiles)


def local(voltages, taps):
    table = jnp.asarray(fourier_rows())
    tiles = corner_turn(voltages, taps, table)
    return correlate(tiles.reshape(4, 64, GROUP, 8, INPUTS))


def solution(mesh):
    in_specs = (P(None, "blk", "freq"), P())
    out_specs = P(None, "freq", "blk", None)
    return jax.shard_map(local, mesh=mesh, in_specs=in_specs, out_specs=out_specs, check_vma=False)
```

```python
import functools
import math

import jax
import jax.numpy as jnp
import ml_dtypes
import numpy as np
from jax import lax
from jax.experimental import pallas as pl
from jax.experimental.pallas import tpu as pltpu
from jax.sharding import PartitionSpec as P

MESH = pl.DeviceIdType.MESH
CHANNELS = 1024
HALF = CHANNELS // 2
INPUTS = 128
FRAMES = 8
GROUP = 32
PITCH = CHANNELS + 8
CHUNK = 256
FIRST = 7
AHEAD = 4
LAG = 8


def fourier_rows():
    n = np.arange(CHANNELS)
    k = np.arange(HALF)
    step = np.float32(2.0 * math.pi / CHANNELS)
    scale = np.float32(1.0 / math.sqrt(CHANNELS))
    phase = (np.outer(k, n) % CHANNELS).astype(np.float32) * step
    cosine = np.cos(phase) * scale
    sine = np.sin(phase) * scale
    sine[0] = np.cos((HALF * n % CHANNELS).astype(np.float32) * step) * scale
    both = np.stack([cosine.reshape(-1, CHUNK, CHANNELS), sine.reshape(-1, CHUNK, CHANNELS)], axis=1)
    return both.reshape(CHANNELS, CHANNELS).astype(ml_dtypes.bfloat16)


def position():
    f = lax.axis_index("freq")
    b = lax.axis_index("blk")
    return (f // 4) % 4, (b // 2) * 2 + f // 16, f % 4, b % 2


def device(x, y, z, c):
    return ((y % 2) * 16 + x * 4 + z, (y // 2) * 2 + c)


def offset(i):
    far = (i + 12) // 16
    r = far * (i - 4)
    return (1 - far) * i + far * (r // 3), far * (1 + r % 3)


def turn_kernel(
    volts, taps, table_hbm, out,
    frames, lines, coeffs, weighted, table, spectra, outbox, inbox,
    load_sem, table_sem, halo_send, halo_recv, plane_send, plane_recv,
    y_send, y_recv, core_send, core_recv, dup_send, dup_recv, keep_sem,
):
    f = lax.axis_index("freq")
    block = lax.axis_index("blk")
    x, y, z, c = position()
    y_lo = y % 2
    here = x * 4 + z
    up = device(x, (y + 1) % 4, z, c)
    down = device(x, (y + 3) % 4, z, c)
    across = device(x, (y + 2) % 4, z, c)
    twin = device(x, y, z, 1 - c)
    after = ((f + 1) % 32, block)
    before = ((f + 31) % 32, block)
    needs_us = ((f + 33 - 2 * c) % 32, block)

    def plane(i, sign):
        dx, dz = offset(i)
        px = (x + 4 + sign * dx) % 4
        pz = (z + 4 + sign * dz) % 4
        return px * 4 + pz, device(px, y, pz, c)

    barrier = pltpu.get_barrier_semaphore()
    for partner in (up, down, across, twin, after, before):
        pl.semaphore_signal(barrier, inc=1, device_id=partner, device_id_type=MESH)

    def greet(i, carry):
        pl.semaphore_signal(barrier, inc=1, device_id=plane(i, 1)[1], device_id_type=MESH)
        return carry

    lax.fori_loop(1, 16, greet, 0)

    def load(p):
        first = pl.multiple_of(((p + 5) % 8) * CHANNELS, CHANNELS)
        return pltpu.make_async_copy(
            volts.at[:, :, pl.ds(first, CHANNELS)], frames.at[p], load_sem.at[p]
        )

    def fetch(t, carry):
        load((3 * c + t) % 8).start()
        return carry

    table_copy = pltpu.make_async_copy(table_hbm, table, table_sem)
    lax.fori_loop(0, 8, fetch, 0)
    table_copy.start()

    coeffs[...] = taps[...].astype(jnp.float32) * (1.0 / 1024.0)

    def narrow(t, carry):
        p = (3 * c + t) % 8
        load(p).wait()

        def body(i, carry):
            rows = pl.ds(pl.multiple_of(i * 16, 16), 16)
            for r in range(2):
                lines[0, p, r, rows, :] = frames[p, r, rows, :].astype(jnp.bfloat16)
            return carry

        return lax.fori_loop(0, INPUTS // 16, body, carry)

    lax.fori_loop(0, 4, narrow, 0)
    pl.semaphore_wait(barrier, 21)
    theirs_first = pl.ds(3 * c, 4)
    halo = pltpu.make_async_remote_copy(
        src_ref=lines.at[0, theirs_first], dst_ref=lines.at[1, theirs_first], send_sem=halo_send,
        recv_sem=halo_recv, device_id=needs_us, device_id_type=MESH,
    )
    halo.start()
    lax.fori_loop(4, 8, narrow, 0)

    def filter_half(frame):
        def body(t, carry):
            rows = pl.ds(pl.multiple_of(t * 16, 16), 16)
            for r in range(2):
                for n in range(0, CHANNELS, 256):
                    cols = slice(n, n + 256)
                    seen = [frame(j, r, rows, cols) for j in range(7)]
                    scale = [jnp.broadcast_to(coeffs[k : k + 1, cols], (16, 256)) for k in range(4)]
                    for s in range(4):
                        total = scale[0] * seen[s]
                        for k in range(1, 4):
                            total = total + scale[k] * seen[s + k]
                        into = pl.ds(pl.multiple_of(r * INPUTS + t * 16, 16), 16)
                        weighted[s, into, cols] = total.astype(jnp.bfloat16)
            return carry

        lax.fori_loop(0, INPUTS // 16, body, 0)

    def late_frame(j, r, rows, cols):
        return frames[(4 + j) % 8, r, rows, cols].astype(jnp.float32)

    live = jnp.where((f + 31 * c) % 62 > 0, 1.0, 0.0).astype(jnp.float32)

    def early_frame(j, r, rows, cols):
        if j < 3:
            return lines[1 - c, j, r, rows, cols].astype(jnp.float32) * live
        return lines[c, j, r, rows, cols].astype(jnp.float32)

    def transform(s):
        rhs = weighted[s]
        re = pl.multiple_of(s * PITCH, 8)
        im = pl.multiple_of((4 + s) * PITCH, 8)
        for q in range(HALF // CHUNK):
            got = lax.dot_general(
                table[q * 2 * CHUNK : (q + 1) * 2 * CHUNK, :], rhs, (((1,), (1,)), ((), ())),
                preferred_element_type=jnp.float32,
            )
            a, b = got[:CHUNK, :INPUTS], got[CHUNK:, :INPUTS]
            cc, d = got[:CHUNK, INPUTS:], got[CHUNK:, INPUTS:]
            k = q * CHUNK
            spectra[pl.ds(re + k, CHUNK), :] = a + d
            spectra[pl.ds(im + k, CHUNK), :] = cc - b
            spectra[pl.ds(re + HALF + k, CHUNK), :] = a - d
            spectra[pl.ds(im + HALF + k, CHUNK), :] = cc + b
            if q == 0:
                spectra[pl.ds(re, 1), :] = a[:1]
                spectra[pl.ds(im, 1), :] = cc[:1]
                spectra[pl.ds(re + CHANNELS, 1), :] = b[:1]
                spectra[pl.ds(im + CHANNELS, 1), :] = d[:1]

    def gather(g, into):
        for k in range(GROUP):
            low = spectra[pl.ds(g * GROUP + k, 8, stride=PITCH), :]
            into[0, k] = low.astype(jnp.bfloat16)
            high = spectra[pl.ds(CHANNELS - g * GROUP - k, 8, stride=PITCH), :]
            into[1, k] = high.astype(jnp.bfloat16)

    def plane_copy(h, i):
        g, to = plane(i, 1)
        return pltpu.make_async_remote_copy(
            src_ref=outbox.at[h, g], dst_ref=inbox.at[h, here], send_sem=plane_send.at[h],
            recv_sem=plane_recv.at[h, here], device_id=to, device_id_type=MESH,
        )

    def collect(h, i):
        g = plane(i, 1)[0]
        gather(g, outbox.at[h, g])

    def forward(h, i):
        j = plane(i, -1)[0]

        def arrive():
            pltpu.make_async_remote_copy(
                src_ref=inbox.at[h, j], dst_ref=inbox.at[h, j], send_sem=plane_send.at[h],
                recv_sem=plane_recv.at[h, j], device_id=twin, device_id_type=MESH,
            ).wait_recv()

        pl.when(i > 0)(arrive)

        theirs = inbox.at[h, j, 1 - y_lo]
        ours = inbox.at[h, j, y_lo]
        slot = out.at[block, h, (y_lo * 16 + j + h * c) % 32]
        for way, (to, chunk) in enumerate(((up, theirs), (down, theirs), (across, ours))):
            pltpu.make_async_remote_copy(
                src_ref=chunk, dst_ref=slot, send_sem=y_send.at[way], recv_sem=y_recv.at[way, h, j],
                device_id=to, device_id_type=MESH,
            ).start()
        pltpu.make_async_remote_copy(
            src_ref=ours, dst_ref=slot, send_sem=core_send, recv_sem=core_recv,
            device_id=twin, device_id_type=MESH,
        ).start()
        pltpu.make_async_copy(ours, slot, keep_sem).start()

    def arrival(way, h, j):
        sender = (y + 3 - 2 * way) % 4 if way < 2 else (y + 2) % 4
        return out.at[(sender // 2) * 2 + c, h, ((sender % 2) * 16 + j + h * c) % 32]

    def duplicate(h, i):
        j = plane(i, -1)[0]
        for way in range(3):
            slot = arrival(way, h, j)
            pltpu.make_async_remote_copy(
                src_ref=slot, dst_ref=slot, send_sem=y_send.at[way], recv_sem=y_recv.at[way, h, j],
                device_id=twin, device_id_type=MESH,
            ).wait_recv()
            pltpu.make_async_remote_copy(
                src_ref=slot, dst_ref=slot, send_sem=dup_send.at[way], recv_sem=dup_recv.at[way],
                device_id=twin, device_id_type=MESH,
            ).start()

    def steps(first, stop, *bodies):
        def run(i, carry):
            for body in bodies:
                body(i)
            return carry

        lax.fori_loop(first, stop, run, 0)

    def step(k):
        forward(k // 16, k % 16)

        @pl.when(k >= LAG)
        def _():
            duplicate((k - LAG) // 16, (k - LAG) % 16)

    def send(m):
        plane_copy(m // 16, m % 16).start()

    filter_half(late_frame)
    table_copy.wait()
    steps(0, 4, transform)
    gather(here, inbox.at[0, here])
    step(0)
    steps(1, FIRST, lambda i: collect(0, i), send)
    steps(FIRST, 16, lambda i: collect(0, i))
    steps(1, FIRST, step)
    halo.wait_send()
    steps(FIRST, FIRST + AHEAD, send)

    halo.wait_recv()
    filter_half(early_frame)
    steps(0, 4, transform, lambda i: step(FIRST + i))
    steps(FIRST + AHEAD, 16, send)
    gather(here, inbox.at[1, here])
    steps(1, 4, lambda i: collect(1, i), lambda i: send(16 + i))
    steps(4, 16, lambda i: collect(1, i))
    steps(FIRST + 4, FIRST + 16, step, lambda k: send(k + 16 - FIRST))
    steps(FIRST + 16, 32, step)
    steps(32 - LAG, 32, lambda k: duplicate(k // 16, k % 16))

    def whole(ref, send_sem, recv_sem):
        return pltpu.make_async_remote_copy(
            src_ref=ref, dst_ref=ref, send_sem=send_sem, recv_sem=recv_sem,
            device_id=twin, device_id_type=MESH,
        )

    for h in range(2):
        whole(outbox.at[h, pl.ds(0, 15)], plane_send.at[h], plane_recv.at[0, 0]).wait_send()
    part = out.at[0, 0]
    for way in range(3):
        whole(part, y_send.at[way], core_recv).wait_send()
        whole(part, dup_send.at[way], core_recv).wait_send()
        whole(part, dup_send.at[way], dup_recv.at[way]).wait_recv()
    whole(part, core_send, core_recv).wait_send()
    whole(part, core_send, core_recv).wait_recv()
    pltpu.make_async_copy(part, part, keep_sem).wait()


def corner_turn(voltages, taps, table):
    bf16 = jnp.bfloat16
    dma = pltpu.SemaphoreType.DMA
    return pl.pallas_call(
        turn_kernel,
        out_shape=pltpu.VMEM((4, 2, 32, GROUP, 8, INPUTS), bf16),
        in_specs=[
            pl.BlockSpec(memory_space=pl.ANY),
            pl.BlockSpec(memory_space=pltpu.VMEM),
            pl.BlockSpec(memory_space=pl.ANY),
        ],
        out_specs=pl.BlockSpec(memory_space=pltpu.VMEM),
        scratch_shapes=[
            pltpu.VMEM((FRAMES, 2, INPUTS, CHANNELS), jnp.int32),
            pltpu.VMEM((2, 8, 2, INPUTS, CHANNELS), bf16),
            pltpu.VMEM((4, CHANNELS), jnp.float32),
            pltpu.VMEM((4, 2 * INPUTS, CHANNELS), bf16),
            pltpu.VMEM((CHANNELS, CHANNELS), bf16),
            pltpu.VMEM((8 * PITCH, INPUTS), jnp.float32),
            pltpu.VMEM((2, 16, 2, GROUP, 8, INPUTS), bf16),
            pltpu.VMEM((2, 16, 2, GROUP, 8, INPUTS), bf16),
            dma((FRAMES,)), dma, dma, dma, dma((2,)), dma((2, 16)),
            dma((3,)), dma((3, 2, 16)), dma, dma, dma((3,)), dma((3,)), dma,
        ],
        compiler_params=pltpu.CompilerParams(
            collective_id=0, has_side_effects=True, vmem_limit_bytes=40 << 20
        ),
        name="corner_turn",
    )(voltages, taps, table)


def correlate_kernel(count, tiles, visible):
    me = lax.axis_index("blk")
    base = pl.program_id(0) * count
    part = lax.broadcasted_iota(jnp.int32, (1, 8, INPUTS), 1)
    sign = jnp.where(part < 4, 0.0625, -0.0625).astype(jnp.float32)
    rows = 64 * 8
    for k in range(count):
        mine = tiles[me, :, :, base + k].astype(jnp.float32).reshape(64, 8, INPUTS)
        rotated = pltpu.roll(mine, 4, axis=1) * sign
        left = jnp.concatenate(
            [(mine * 0.0625).reshape(rows, INPUTS), rotated.reshape(rows, INPUTS)], axis=1
        ).astype(jnp.bfloat16)
        for b in range(0, 4, 2):
            right = jnp.concatenate(
                [tiles[b, :, :, base + k].reshape(rows, INPUTS), tiles[b + 1, :, :, base + k].reshape(rows, INPUTS)], axis=1
            )
            both = lax.dot_general(
                left, right, (((0,), (0,)), ((), ())), preferred_element_type=jnp.float32
            )
            visible[0, k, :, b * INPUTS : (b + 2) * INPUTS] = both[:INPUTS]
            visible[1, k, :, b * INPUTS : (b + 2) * INPUTS] = both[INPUTS:]


def correlate(tiles, count=8):
    return pl.pallas_call(
        functools.partial(correlate_kernel, count),
        grid=(GROUP // count,),
        in_specs=[pl.BlockSpec(memory_space=pltpu.VMEM)],
        out_specs=pl.BlockSpec((2, count, INPUTS, 4 * INPUTS), lambda k: (0, k, 0, 0)),
        out_shape=jax.ShapeDtypeStruct((2, GROUP, INPUTS, 4 * INPUTS), jnp.float32),
        compiler_params=pltpu.CompilerParams(vmem_limit_bytes=40 << 20),
        name="correlate",
    )(tiles)


def local(voltages, taps):
    table = jnp.asarray(fourier_rows())
    tiles = corner_turn(voltages, taps, table)
    return correlate(pltpu.with_memory_space_constraint(tiles, pltpu.VMEM))


def solution(mesh):
    in_specs = (P(None, "blk", "freq"), P())
    out_specs = P(None, "freq", "blk", None)
    return jax.shard_map(local, mesh=mesh, in_specs=in_specs, out_specs=out_specs, check_vma=False)
```

```python
import functools
import math

import jax
import jax.numpy as jnp
import ml_dtypes
import numpy as np
from jax import lax
from jax.experimental import pallas as pl
from jax.experimental.pallas import tpu as pltpu
from jax.sharding import PartitionSpec as P

MESH = pl.DeviceIdType.MESH
CHANNELS = 1024
HALF = CHANNELS // 2
INPUTS = 128
FRAMES = 8
GROUP = 32
PITCH = CHANNELS + 8
CHUNK = 256
FIRST = 7
AHEAD = 4
LAG = 8


def fourier_rows():
    n = np.arange(CHANNELS)
    k = np.arange(HALF)
    step = np.float32(2.0 * math.pi / CHANNELS)
    scale = np.float32(1.0 / math.sqrt(CHANNELS))
    phase = (np.outer(k, n) % CHANNELS).astype(np.float32) * step
    cosine = np.cos(phase) * scale
    sine = np.sin(phase) * scale
    sine[0] = np.cos((HALF * n % CHANNELS).astype(np.float32) * step) * scale
    both = np.stack([cosine.reshape(-1, CHUNK, CHANNELS), sine.reshape(-1, CHUNK, CHANNELS)], axis=1)
    return both.reshape(CHANNELS, CHANNELS).astype(ml_dtypes.bfloat16)


def position():
    f = lax.axis_index("freq")
    b = lax.axis_index("blk")
    return (f // 4) % 4, (b // 2) * 2 + f // 16, f % 4, b % 2


def device(x, y, z, c):
    return ((y % 2) * 16 + x * 4 + z, (y // 2) * 2 + c)


def offset(i):
    far = (i + 12) // 16
    r = far * (i - 4)
    return (1 - far) * i + far * (r // 3), far * (1 + (r + 1) % 3)


def turn_kernel(
    volts, taps, table_hbm, out,
    frames, lines, coeffs, weighted, table, spectra, outbox, inbox,
    load_sem, table_sem, halo_send, halo_recv, plane_send, plane_recv,
    y_send, y_recv, core_send, core_recv, dup_send, dup_recv, keep_sem,
):
    f = lax.axis_index("freq")
    block = lax.axis_index("blk")
    x, y, z, c = position()
    y_lo = y % 2
    here = x * 4 + z
    up = device(x, (y + 1) % 4, z, c)
    down = device(x, (y + 3) % 4, z, c)
    across = device(x, (y + 2) % 4, z, c)
    twin = device(x, y, z, 1 - c)
    after = ((f + 1) % 32, block)
    before = ((f + 31) % 32, block)
    needs_us = ((f + 33 - 2 * c) % 32, block)

    def plane(i, sign):
        dx, dz = offset(i)
        px = (x + 4 + sign * dx) % 4
        pz = (z + 4 + sign * dz) % 4
        return px * 4 + pz, device(px, y, pz, c)

    barrier = pltpu.get_barrier_semaphore()
    for partner in (up, down, across, twin, after, before):
        pl.semaphore_signal(barrier, inc=1, device_id=partner, device_id_type=MESH)

    def greet(i, carry):
        pl.semaphore_signal(barrier, inc=1, device_id=plane(i, 1)[1], device_id_type=MESH)
        return carry

    lax.fori_loop(1, 16, greet, 0)

    def load(p):
        first = pl.multiple_of(((p + 5) % 8) * CHANNELS, CHANNELS)
        return pltpu.make_async_copy(
            volts.at[:, :, pl.ds(first, CHANNELS)], frames.at[p], load_sem.at[p]
        )

    def fetch(t, carry):
        load((3 * c + t) % 8).start()
        return carry

    table_copy = pltpu.make_async_copy(table_hbm, table, table_sem)
    lax.fori_loop(0, 8, fetch, 0)
    table_copy.start()

    coeffs[...] = taps[...].astype(jnp.float32) * (1.0 / 1024.0)

    def narrow(t, carry):
        p = (3 * c + t) % 8
        load(p).wait()

        def body(i, carry):
            rows = pl.ds(pl.multiple_of(i * 16, 16), 16)
            for r in range(2):
                lines[0, p, r, rows, :] = frames[p, r, rows, :].astype(jnp.bfloat16)
            return carry

        return lax.fori_loop(0, INPUTS // 16, body, carry)

    lax.fori_loop(0, 4, narrow, 0)
    pl.semaphore_wait(barrier, 21)
    theirs_first = pl.ds(3 * c, 4)
    halo = pltpu.make_async_remote_copy(
        src_ref=lines.at[0, theirs_first], dst_ref=lines.at[1, theirs_first], send_sem=halo_send,
        recv_sem=halo_recv, device_id=needs_us, device_id_type=MESH,
    )
    halo.start()
    lax.fori_loop(4, 8, narrow, 0)

    def filter_half(frame):
        def body(t, carry):
            rows = pl.ds(pl.multiple_of(t * 16, 16), 16)
            for r in range(2):
                for n in range(0, CHANNELS, 256):
                    cols = slice(n, n + 256)
                    seen = [frame(j, r, rows, cols) for j in range(7)]
                    scale = [jnp.broadcast_to(coeffs[k : k + 1, cols], (16, 256)) for k in range(4)]
                    for s in range(4):
                        total = scale[0] * seen[s]
                        for k in range(1, 4):
                            total = total + scale[k] * seen[s + k]
                        into = pl.ds(pl.multiple_of(r * INPUTS + t * 16, 16), 16)
                        weighted[s, into, cols] = total.astype(jnp.bfloat16)
            return carry

        lax.fori_loop(0, INPUTS // 16, body, 0)

    def late_frame(j, r, rows, cols):
        return frames[(4 + j) % 8, r, rows, cols].astype(jnp.float32)

    live = jnp.where((f + 31 * c) % 62 > 0, 1.0, 0.0).astype(jnp.float32)

    def early_frame(j, r, rows, cols):
        if j < 3:
            return lines[1 - c, j, r, rows, cols].astype(jnp.float32) * live
        return lines[c, j, r, rows, cols].astype(jnp.float32)

    def transform(s):
        rhs = weighted[s]
        re = pl.multiple_of(s * PITCH, 8)
        im = pl.multiple_of((4 + s) * PITCH, 8)
        for q in range(HALF // CHUNK):
            got = lax.dot_general(
                table[q * 2 * CHUNK : (q + 1) * 2 * CHUNK, :], rhs, (((1,), (1,)), ((), ())),
                preferred_element_type=jnp.float32,
            )
            a, b = got[:CHUNK, :INPUTS], got[CHUNK:, :INPUTS]
            cc, d = got[:CHUNK, INPUTS:], got[CHUNK:, INPUTS:]
            k = q * CHUNK
            spectra[pl.ds(re + k, CHUNK), :] = a + d
            spectra[pl.ds(im + k, CHUNK), :] = cc - b
            spectra[pl.ds(re + HALF + k, CHUNK), :] = a - d
            spectra[pl.ds(im + HALF + k, CHUNK), :] = cc + b
            if q == 0:
                spectra[pl.ds(re, 1), :] = a[:1]
                spectra[pl.ds(im, 1), :] = cc[:1]
                spectra[pl.ds(re + CHANNELS, 1), :] = b[:1]
                spectra[pl.ds(im + CHANNELS, 1), :] = d[:1]

    def gather(g, into):
        for k in range(GROUP):
            low = spectra[pl.ds(g * GROUP + k, 8, stride=PITCH), :]
            into[0, k] = low.astype(jnp.bfloat16)
            high = spectra[pl.ds(CHANNELS - g * GROUP - k, 8, stride=PITCH), :]
            into[1, k] = high.astype(jnp.bfloat16)

    def plane_copy(h, i):
        g, to = plane(i, 1)
        return pltpu.make_async_remote_copy(
            src_ref=outbox.at[h, g], dst_ref=inbox.at[h, here], send_sem=plane_send.at[h],
            recv_sem=plane_recv.at[h, here], device_id=to, device_id_type=MESH,
        )

    def collect(h, i):
        g = plane(i, 1)[0]
        gather(g, outbox.at[h, g])

    def forward(h, i):
        j = plane(i, -1)[0]

        def arrive():
            pltpu.make_async_remote_copy(
                src_ref=inbox.at[h, j], dst_ref=inbox.at[h, j], send_sem=plane_send.at[h],
                recv_sem=plane_recv.at[h, j], device_id=twin, device_id_type=MESH,
            ).wait_recv()

        pl.when(i > 0)(arrive)

        theirs = inbox.at[h, j, 1 - y_lo]
        ours = inbox.at[h, j, y_lo]
        slot = out.at[block, h, (y_lo * 16 + j + h * c) % 32]
        for way, (to, chunk) in enumerate(((up, theirs), (down, theirs), (across, ours))):
            pltpu.make_async_remote_copy(
                src_ref=chunk, dst_ref=slot, send_sem=y_send.at[way], recv_sem=y_recv.at[way, h, j],
                device_id=to, device_id_type=MESH,
            ).start()
        pltpu.make_async_remote_copy(
            src_ref=ours, dst_ref=slot, send_sem=core_send, recv_sem=core_recv,
            device_id=twin, device_id_type=MESH,
        ).start()
        pltpu.make_async_copy(ours, slot, keep_sem).start()

    def arrival(way, h, j):
        sender = (y + 3 - 2 * way) % 4 if way < 2 else (y + 2) % 4
        return out.at[(sender // 2) * 2 + c, h, ((sender % 2) * 16 + j + h * c) % 32]

    def duplicate(h, i):
        j = plane(i, -1)[0]
        for way in range(3):
            slot = arrival(way, h, j)
            pltpu.make_async_remote_copy(
                src_ref=slot, dst_ref=slot, send_sem=y_send.at[way], recv_sem=y_recv.at[way, h, j],
                device_id=twin, device_id_type=MESH,
            ).wait_recv()
            pltpu.make_async_remote_copy(
                src_ref=slot, dst_ref=slot, send_sem=dup_send.at[way], recv_sem=dup_recv.at[way],
                device_id=twin, device_id_type=MESH,
            ).start()

    def steps(first, stop, *bodies):
        def run(i, carry):
            for body in bodies:
                body(i)
            return carry

        lax.fori_loop(first, stop, run, 0)

    def step(k):
        forward(k // 16, k % 16)

        @pl.when(k >= LAG)
        def _():
            duplicate((k - LAG) // 16, (k - LAG) % 16)

    def send(m):
        plane_copy(m // 16, m % 16).start()

    filter_half(late_frame)
    table_copy.wait()
    steps(0, 4, transform)
    gather(here, inbox.at[0, here])
    step(0)
    steps(1, FIRST, lambda i: collect(0, i), send)
    steps(FIRST, 16, lambda i: collect(0, i))
    steps(1, FIRST, step)
    halo.wait_send()
    steps(FIRST, FIRST + AHEAD, send)

    halo.wait_recv()
    filter_half(early_frame)
    steps(0, 4, transform, lambda i: step(FIRST + i))
    steps(FIRST + AHEAD, 16, send)
    gather(here, inbox.at[1, here])
    steps(1, 4, lambda i: collect(1, i), lambda i: send(16 + i))
    steps(4, 16, lambda i: collect(1, i))
    steps(FIRST + 4, FIRST + 16, step, lambda k: send(k + 16 - FIRST))
    steps(FIRST + 16, 32, step)
    steps(32 - LAG, 32, lambda k: duplicate(k // 16, k % 16))

    def whole(ref, send_sem, recv_sem):
        return pltpu.make_async_remote_copy(
            src_ref=ref, dst_ref=ref, send_sem=send_sem, recv_sem=recv_sem,
            device_id=twin, device_id_type=MESH,
        )

    for h in range(2):
        whole(outbox.at[h, pl.ds(0, 15)], plane_send.at[h], plane_recv.at[0, 0]).wait_send()
    part = out.at[0, 0]
    for way in range(3):
        whole(part, y_send.at[way], core_recv).wait_send()
        whole(part, dup_send.at[way], core_recv).wait_send()
        whole(part, dup_send.at[way], dup_recv.at[way]).wait_recv()
    whole(part, core_send, core_recv).wait_send()
    whole(part, core_send, core_recv).wait_recv()
    pltpu.make_async_copy(part, part, keep_sem).wait()


def corner_turn(voltages, taps, table):
    bf16 = jnp.bfloat16
    dma = pltpu.SemaphoreType.DMA
    return pl.pallas_call(
        turn_kernel,
        out_shape=pltpu.VMEM((4, 2, 32, GROUP, 8, INPUTS), bf16),
        in_specs=[
            pl.BlockSpec(memory_space=pl.ANY),
            pl.BlockSpec(memory_space=pltpu.VMEM),
            pl.BlockSpec(memory_space=pl.ANY),
        ],
        out_specs=pl.BlockSpec(memory_space=pltpu.VMEM),
        scratch_shapes=[
            pltpu.VMEM((FRAMES, 2, INPUTS, CHANNELS), jnp.int32),
            pltpu.VMEM((2, 8, 2, INPUTS, CHANNELS), bf16),
            pltpu.VMEM((4, CHANNELS), jnp.float32),
            pltpu.VMEM((4, 2 * INPUTS, CHANNELS), bf16),
            pltpu.VMEM((CHANNELS, CHANNELS), bf16),
            pltpu.VMEM((8 * PITCH, INPUTS), jnp.float32),
            pltpu.VMEM((2, 16, 2, GROUP, 8, INPUTS), bf16),
            pltpu.VMEM((2, 16, 2, GROUP, 8, INPUTS), bf16),
            dma((FRAMES,)), dma, dma, dma, dma((2,)), dma((2, 16)),
            dma((3,)), dma((3, 2, 16)), dma, dma, dma((3,)), dma((3,)), dma,
        ],
        compiler_params=pltpu.CompilerParams(
            collective_id=0, has_side_effects=True, vmem_limit_bytes=40 << 20
        ),
        name="corner_turn",
    )(voltages, taps, table)


def correlate_kernel(count, tiles, visible):
    me = lax.axis_index("blk")
    base = pl.program_id(0) * count
    part = lax.broadcasted_iota(jnp.int32, (1, 8, INPUTS), 1)
    sign = jnp.where(part < 4, 0.0625, -0.0625).astype(jnp.float32)
    rows = 64 * 8
    for k in range(count):
        mine = tiles[me, :, :, base + k].astype(jnp.float32).reshape(64, 8, INPUTS)
        rotated = pltpu.roll(mine, 4, axis=1) * sign
        left = jnp.concatenate(
            [(mine * 0.0625).reshape(rows, INPUTS), rotated.reshape(rows, INPUTS)], axis=1
        ).astype(jnp.bfloat16)
        for b in range(0, 4, 2):
            right = jnp.concatenate(
                [tiles[b, :, :, base + k].reshape(rows, INPUTS), tiles[b + 1, :, :, base + k].reshape(rows, INPUTS)], axis=1
            )
            both = lax.dot_general(
                left, right, (((0,), (0,)), ((), ())), preferred_element_type=jnp.float32
            )
            visible[0, k, :, b * INPUTS : (b + 2) * INPUTS] = both[:INPUTS]
            visible[1, k, :, b * INPUTS : (b + 2) * INPUTS] = both[INPUTS:]


def correlate(tiles, count=8):
    return pl.pallas_call(
        functools.partial(correlate_kernel, count),
        grid=(GROUP // count,),
        in_specs=[pl.BlockSpec(memory_space=pltpu.VMEM)],
        out_specs=pl.BlockSpec((2, count, INPUTS, 4 * INPUTS), lambda k: (0, k, 0, 0)),
        out_shape=jax.ShapeDtypeStruct((2, GROUP, INPUTS, 4 * INPUTS), jnp.float32),
        compiler_params=pltpu.CompilerParams(vmem_limit_bytes=40 << 20),
        name="correlate",
    )(tiles)


def local(voltages, taps):
    table = jnp.asarray(fourier_rows())
    tiles = corner_turn(voltages, taps, table)
    return correlate(pltpu.with_memory_space_constraint(tiles, pltpu.VMEM))


def solution(mesh):
    in_specs = (P(None, "blk", "freq"), P())
    out_specs = P(None, "freq", "blk", None)
    return jax.shard_map(local, mesh=mesh, in_specs=in_specs, out_specs=out_specs, check_vma=False)
```
